512 devices in a mesh: slab: 16 (over x, z_hi, core), energy: 32 (over y, z_lo).
Axes of the slice: x: 4, y: 4, z: 16 (z_hi: 2, z_lo: 8; z = z_hi * 8 + z_lo), core: 2. Of those that a mesh axis runs over, the one named last changes fastest.
Arguments:
- hamiltonian: float32 [16, 256, 256], P('slab'), may hold values from -0.375 to 0.375
- coupling: float32 [16, 256, 256], P('slab'), may hold values from -0.375 to 0.375
- pattern: int32 [16, 4, 4], P('slab'), may hold values 0 or 1
- energy: float32 [32], P('energy'), may hold values from -2 to 2
- broadening: float32 [32], P('energy'), may hold values from 0.03 to 0.1
- weights: float32 [32], P('energy'), may hold values from 0.5 to 1.5
Outputs:
- density: float32 [16, 256, 256], P('slab', 'energy')
The draws below stay inside these ranges and needn't reach their ends.
All inputs are finite; a program needn't handle non-finite values. No bound on the sum of `pattern` on one device may be relied on, other than what follows from the above.
Results may differ from the reference program's by a relative error of at most 0.023.
Values may be sent and summed in bfloat16 or wider, within the bound.
No kernel may reach another device: no remote copies, remote signals or barrier semaphores. Data moves between devices by JAX's collectives and lax.ppermute only.
A program may use at most 64 MiB of HBM per device.

```python
import math
import jax
import jax.numpy as jnp
from jax import lax

ORB = 256
NB = 4
SLABS = 16
ENERGIES = 32


def with_ends(array, rng, smallest, top_value):
    longest = array.shape.index(max(array.shape))
    spots = []
    for shift in (0, 1):
        where = [jax.random.randint(jax.random.fold_in(rng, axis), (), 0, length) for axis, length in enumerate(array.shape)]
        where[longest] = (where[longest] + shift) % array.shape[longest]
        spots.append(tuple(where))
    return array.at[spots[0]].set(smallest).at[spots[1]].set(top_value)


def block_scale(own_key, extent, pieces, low, top_value):
    gain = 1.0
    for dim, blocks in pieces:
        steps = jax.random.uniform(jax.random.fold_in(jax.random.fold_in(own_key, 6), dim), (blocks,), jnp.float32, low / len(pieces), top_value / len(pieces))
        gain = gain * jnp.repeat(jnp.exp(steps), extent[dim] // blocks).reshape((-1,) + (1,) * (len(extent) - 1 - dim))
    return gain


def scatter_about(own_key, shape, deviation, bound, pieces=(), kind=jnp.bfloat16):
    loudness = block_scale(own_key, shape, pieces, -0.22, 0.18) if pieces else 1.0
    array = jax.random.normal(own_key, shape, jnp.float32) * deviation * loudness
    return jnp.minimum(jnp.maximum(array, -bound), bound).astype(kind)


def setup_inputs(seed: int = 0) -> dict:
    key_of = jax.random.split(jax.random.key(seed), 7)
    hamiltonian = scatter_about(key_of[0], (SLABS, ORB, ORB), ORB ** -0.5, 0.375, ((0, 16),), jnp.float32)
    coupling = scatter_about(key_of[1], (SLABS, ORB, ORB), ORB ** -0.5, 0.375, ((0, 16),), jnp.float32)
    pattern = with_ends((jax.random.randint(key_of[2], (SLABS, NB, NB), 0, 4) < 3).astype(jnp.int32), jax.random.fold_in(key_of[2], 1), 0, 1)
    energy = jnp.clip(jax.random.uniform(key_of[3], (ENERGIES,), jnp.float32, -2.0, 2.0) * block_scale(key_of[3], (ENERGIES,), ((0, 32),), -0.4, 0.0), -2.0, 2.0)
    broadening = jnp.clip(jnp.exp(math.log(0.1) - 1.2039728 * jax.random.uniform(key_of[4], (ENERGIES,), jnp.float32) ** block_scale(key_of[4], (ENERGIES,), ((0, 32),), -0.2, 0.2)), 0.03, 0.1)
    weights = jnp.clip(0.5 + 1.0 * jax.random.uniform(key_of[5], (ENERGIES,), jnp.float32) ** block_scale(key_of[5], (ENERGIES,), ((0, 32),), -0.2, 0.2), 0.5, 1.5)
    return {"hamiltonian": hamiltonian, "coupling": coupling, "pattern": pattern, "energy": energy, "broadening": broadening, "weights": weights}


def reference(hamiltonian, coupling, pattern, energy, broadening, weights):
    slabs, size, _ = hamiltonian.shape
    blocks = pattern.shape[1]
    width = size // blocks
    tiles = jnp.broadcast_to(pattern.astype(jnp.float32)[:, :, None, :, None], (slabs, blocks, width, blocks, width)).reshape(slabs, size, size)
    masked = coupling * tiles
    ham_sym = 0.5 * (hamiltonian + jnp.swapaxes(hamiltonian, 1, 2))
    count = energy.shape[0]
    identity = jnp.eye(size, dtype=jnp.float32)
    nothing = jnp.zeros((size, size), jnp.float32)
    lead = jnp.broadcast_to(jnp.stack([nothing, -0.5 * identity]), (count, 2, size, size))
    target = jnp.broadcast_to(jnp.concatenate([identity, nothing], axis=0), (count, 2 * size, size))

    def advance(handed, inputs):
        ham_one, coup = inputs
        sigma = jnp.einsum('ij,epjk,lk->epil', coup, handed, coup, precision=lax.Precision.HIGHEST)
        real_part = energy[:, None, None] * identity - ham_one - sigma[:, 0]
        imag_part = broadening[:, None, None] * identity - sigma[:, 1]
        upper = jnp.concatenate([real_part, -imag_part], axis=2)
        lower = jnp.concatenate([imag_part, real_part], axis=2)
        embed = jnp.concatenate([upper, lower], axis=1)
        solved = jnp.linalg.solve(embed, target)
        real_green = solved[:, :size]
        imag_green = solved[:, size:]
        density = 4.0 / count * jnp.einsum('e,eij->ij', weights, -imag_green, precision=lax.Precision.HIGHEST)
        rounded = jnp.stack([real_green, imag_green], axis=1).astype(jnp.bfloat16)
        following = lax.optimization_barrier(rounded).astype(jnp.float32)
        return (following, density)
    _, density = lax.scan(advance, lead, (ham_sym, masked))
    return density
```

```python
import functools

import jax
import jax.numpy as jnp
from jax import lax
from jax.experimental import pallas as pl
from jax.experimental.pallas import tpu as pltpu
from jax.sharding import PartitionSpec as P

LEAD_SCALE = 0.5
CHUNK = 4
LINE = 8
F32=jnp.float32; BF=jnp.bfloat16
HI=lax.Precision.HIGHEST
NS=32

def eye(n, m=None):
    m = n if m is None else m
    return (lax.broadcasted_iota(jnp.int32,(n,m),0)==lax.broadcasted_iota(jnp.int32,(n,m),1)).astype(F32)

def sweep(br, bi, width):
    lanes = br.shape[1]
    two = lanes > width
    half = lax.broadcasted_iota(jnp.int32,(width,lanes),1)//width*width if two else None
    def column(x,k):
        if two:
            return jnp.take_along_axis(x, half+k, axis=1)
        return x[:,k:k+1]
    for k in range(width):
        rr = br[k:k+1,:]; ri = bi[k:k+1,:]
        cr = column(br,k); ci = column(bi,k)
        pr = cr[k:k+1,:]+1.0; pi = ci[k:k+1,:]
        den = 1.0/(pr*pr+pi*pi)
        qr = pr*den; qi = -pi*den
        sr = qr*rr-qi*ri; si = qr*ri+qi*rr
        br = br - cr*sr + ci*si
        bi = bi - cr*si - ci*sr
    return br, bi

def dot(a,b,ca,cb):
    return lax.dot_general(a,b,(((ca,),(cb,)),((),())),precision=HI,preferred_element_type=F32)

def clear(mats, off, n):
    for K in range(0,n,NS):
        rows=pl.ds(off+K,NS); cols=pl.ds(off,n)
        br = [r[rows,cols] for r,_ in mats]; bi=[i[rows,cols] for _,i in mats]
        dr = jnp.concatenate([x[:,K:K+NS] for x in br],1); di = jnp.concatenate([x[:,K:K+NS] for x in bi],1)
        dr, di = sweep(dr,di,NS)
        for j,(r,i) in enumerate(mats):
            pr = eye(NS)-dr[:,j*NS:(j+1)*NS]; pi = -di[:,j*NS:(j+1)*NS]
            left = jnp.concatenate([jnp.concatenate([pr,-pi],1),jnp.concatenate([pi,pr],1)],0)
            solved = dot(left,jnp.concatenate([br[j],bi[j]],0),1,0)
            wide = jnp.concatenate([jnp.concatenate([br[j],-bi[j]],0),jnp.concatenate([bi[j],br[j]],0)],1)
            d = dot(wide,solved,0,0)
            r[off:off+n,off:off+n] -= d[:n]
            i[off:off+n,off:off+n] -= d[n:]

def cdot(ar,ai,br,bi,ca,cb):
    lr=jnp.concatenate([ar,-ai],ca); li=jnp.concatenate([ai,ar],ca)
    right=jnp.concatenate([br,bi],cb)
    return dot(lr,right,ca,cb), dot(li,right,ca,cb)

def invert(mats):
    n = mats[0][0].shape[0]; h=n//2
    clear(mats,0,h)
    keep=[]
    for r,i in mats:
        pr=eye(h)-r[:h,:h]; pi=-i[:h,:h]
        xr=r[:h,h:]; xi=i[:h,h:]
        tr,ti=cdot(pr,pi,xr,xi,1,0)
        sr,si=cdot(xr,xi,tr,ti,0,0)
        r[h:,h:]-=sr; i[h:,h:]-=si
        keep.append((pr,pi,tr,ti))
    clear(mats,h,h)
    for (r,i),(pr,pi,tr,ti) in zip(mats,keep):
        gr=eye(h)-r[h:,h:]; gi=-i[h:,h:]
        qr,qi=cdot(tr,ti,gr,gi,1,0)
        ur,ui=cdot(qr,qi,tr,ti,1,1)
        r[:h,:h]=pr+ur; i[:h,:h]=pi+ui
        r[:h,h:]=-qr; i[:h,h:]=-qi
        r[h:,:h]=-qr.T; i[h:,:h]=-qi.T
        r[h:,h:]=gr; i[h:,h:]=gi


def bdot(a, b, ca, cb):
    return lax.dot_general(a, b, (((ca,), (cb,)), ((), ())), preferred_element_type=F32)


def split(x):
    high = x.astype(BF)
    rest = x - high.astype(F32)
    middle = rest.astype(BF)
    return high, middle, (rest - middle.astype(F32)).astype(BF)


def plane_kernel(step, pos, point, slabs, received, weighted, handed_out, ar, ai, dr, di, handed):
    active = pos[0] == step
    size = slabs.shape[-1]

    @pl.when(jnp.logical_not(active))
    def _():
        weighted[...] = jnp.zeros_like(weighted)
        handed_out[...] = jnp.zeros_like(handed_out)

    @pl.when(active)
    def _():
        if step == 0:
            handed[0] = jnp.zeros((size, size), BF)
            handed[1] = (-LEAD_SCALE * eye(size)).astype(BF)
        else:
            handed[...] = received[...]

        @pl.loop(0, CHUNK)
        def _(j):
            v = slabs[j, 1]
            for part, ref in ((0, ar), (1, ai)):
                once = bdot(v, handed[part], 1, 0)
                sigma = sum(bdot(p, v, 1, 1) for p in split(once)[::-1])
                sigma = 0.5 * (sigma + sigma.T)
                if part == 0:
                    dr[...] = point[0] * eye(size) - slabs[j, 0].astype(F32) - sigma
                    ref[...] = dr[...] - eye(size)
                else:
                    di[...] = point[1] * eye(size) - sigma
                    ref[...] = di[...]
            invert([(ar, ai)])

            @pl.loop(0, 2)
            def _(_):
                xr, xi = ar[...], ai[...]
                er, ei = cdot(dr[...], di[...], xr, xi, 1, 0)
                ur, ui = cdot(xr, xi, eye(size) - er, -ei, 1, 0)
                ar[...] = xr + ur
                ai[...] = xi + ui

            handed[0] = ar[...].astype(BF)
            handed[1] = ai[...].astype(BF)

            @pl.when(pos[1] == j)
            def _():
                weighted[...] = (point[2] * (0.0 - ai[...])).astype(weighted.dtype)

        handed_out[...] = handed[...]


def run_plane(step, pos, point, slabs, received):
    size = slabs.shape[-1]
    whole = jax.ShapeDtypeStruct((2, size, size), BF)
    return pl.pallas_call(
        functools.partial(plane_kernel, step),
        out_shape=[jax.ShapeDtypeStruct((size, size), BF), whole],
        in_specs=[pl.BlockSpec(memory_space=pltpu.SMEM)] * 2 + [pl.BlockSpec(memory_space=pltpu.VMEM)] * 2,
        out_specs=[pl.BlockSpec(memory_space=pltpu.VMEM)] * 2,
        scratch_shapes=[pltpu.VMEM((size, size), F32)] * 4 + [pltpu.VMEM((2, size, size), BF)],
        compiler_params=pltpu.CompilerParams(vmem_limit_bytes=32 * 1024 * 1024),
        cost_estimate=pl.CostEstimate(flops=400 * size**3, bytes_accessed=2 << 20, transcendentals=0),
    )(pos, point, slabs, received)


def summed_on_arrival(array, axis):
    size = lax.axis_size(axis)
    parts = lax.all_to_all(array.reshape(size, -1, array.shape[-1]), axis, 0, 0, tiled=True)
    return jnp.sum(parts.astype(F32), axis=0)


def body(hamiltonian, coupling, pattern, energy, broadening, weights):
    _, size, _ = hamiltonian.shape
    blocks = pattern.shape[1]
    width = size // blocks
    chain = lax.axis_size("slab")
    count = lax.axis_size("energy")
    tiles = jnp.broadcast_to(
        pattern[0].astype(F32)[:, None, :, None], (blocks, width, blocks, width)
    ).reshape(size, size)
    masked = coupling[0] * tiles
    ham_sym = 0.5 * (hamiltonian[0] + hamiltonian[0].T)
    own = jnp.stack([ham_sym, masked]).astype(BF)

    position = lax.axis_index("slab")
    chunk = position // CHUNK
    rank = position % CHUNK

    def flip_core(x):
        return lax.ppermute(x, "slab", [(i, i ^ 1) for i in range(chain)])

    mirrored = []
    for s in range(chain):
        for e in range(count):
            mirrored.append((s * count + e, (s ^ 2) * count + e // LINE * LINE + (LINE - 1 - e % LINE)))
    other = lax.ppermute(own, ("slab", "energy"), mirrored)
    near = flip_core(own)
    far = flip_core(other)
    even = rank % 2 == 0
    here = (jnp.where(even, own, near), jnp.where(even, near, own))
    there = (jnp.where(even, other, far), jnp.where(even, far, other))
    low = rank < 2
    slabs = jnp.stack(
        [jnp.where(low, here[0], there[0]), jnp.where(low, here[1], there[1]),
         jnp.where(low, there[0], here[0]), jnp.where(low, there[1], here[1])]
    )

    pos = jnp.stack([chunk, rank]).astype(jnp.int32)
    point = jnp.stack([energy[0], broadening[0], weights[0] * (4.0 / count)])
    received = jnp.zeros((2, size, size), BF)
    density = jnp.zeros((size, size), BF)
    for step in range(chain // CHUNK):
        weighted, handed = run_plane(step, pos, point, slabs, received)
        density = density + weighted
        if step + 1 < chain // CHUNK:
            received = lax.ppermute(
                handed, "slab", [(i, i + CHUNK) for i in range(step * CHUNK, (step + 1) * CHUNK)]
            )
    return summed_on_arrival(density, "energy")[None]


def solution(mesh):
    in_specs = (
        P("slab", None, None),
        P("slab", None, None),
        P("slab", None, None),
        P("energy"),
        P("energy"),
        P("energy"),
    )
    out_specs = P("slab", "energy", None)
    return jax.shard_map(body, mesh=mesh, in_specs=in_specs, out_specs=out_specs, check_vma=False)
```
